256 devices in a mesh: ctx: 16 (over z, core), exp: 16 (over y, x).
Axes of the slice: x: 4, y: 4, z: 8, core: 2. Of those that a mesh axis runs over, the one named last changes fastest.
Arguments:
- u_in: bfloat16 [2048, 16384], P('ctx', 'exp'), may hold values from -6 to 6
- z_in: bfloat16 [2048, 16384], P('ctx', 'exp'), may hold values from -6 to 6
- delta: float32 [2048, 16384], P('ctx', 'exp'), may hold values from 0.25 to 2
- bc_proj: float32 [32, 2048], P(None, 'ctx'), may hold values from -0.6 to 0.6
- a_rate: float32 [16, 16384], P(None, 'exp'), may hold values from 9.765625e-07 to 0.2
- d_skip: float32 [16384], P('exp'), may hold values from 0.5 to 1.5
- w_out: bfloat16 [16384, 8192], P('exp', 'ctx'), may hold values from -0.046875 to 0.046875
Outputs:
- mixer_out: bfloat16 [2048, 8192], P('exp', 'ctx')
The draws below stay inside these ranges and needn't reach their ends.
All inputs are finite; a program needn't handle non-finite values.
Results may differ from the reference program's by a relative error of at most 0.0048.
Values may be sent and summed in bfloat16 or wider, within the bound.
No kernel may reach another device: no remote copies, remote signals or barrier semaphores. Data moves between devices by JAX's collectives and lax.ppermute only.
A program may use at most 128 MiB of HBM per device.

```python
import math
import jax
import jax.numpy as jnp
from jax import lax

D = 8192
NSTATE = 16
LEN = 2048
CH = 16384


def level_of(own_key, extent, cuts, smallest, high):
    def one(position, shards_of):
        draws = jax.random.uniform(jax.random.fold_in(jax.random.fold_in(own_key, 6), position), (shards_of,), jnp.float32, smallest / len(cuts), high / len(cuts))
        return jnp.repeat(jnp.exp(draws), extent[position] // shards_of).reshape((-1,) + (1,) * (len(extent) - position - 1))

    gain = one(*cuts[0])
    for cut in cuts[1:]:
        gain = gain * one(*cut)
    return gain


def gaussian(own_key, shape, spread, bound, cuts=(), held_as=jnp.bfloat16):
    array = jax.random.normal(own_key, shape, jnp.float32) * spread
    if len(cuts) > 0:
        array = level_of(own_key, shape, cuts, -0.22, 0.18) * array
    return jnp.clip(array, min=-bound, max=bound).astype(held_as)


def setup_inputs(seed: int = 0) -> dict:
    streams_of = jax.random.split(jax.random.key(seed), 8)
    return {
        "u_in": gaussian(streams_of[0], (LEN, CH), 1.0, 6.0, ((0, 16), (1, 16))),
        "z_in": gaussian(streams_of[1], (LEN, CH), 1.0, 6.0, ((0, 16), (1, 16))),
        "delta": jnp.clip(jnp.exp(math.log(2.0) - 2.0794415 * jax.random.uniform(streams_of[2], (LEN, CH), jnp.float32) ** level_of(streams_of[2], (LEN, CH), ((0, 16), (1, 16)), -0.2, 0.2)), 0.25, 2.0),
        "bc_proj": gaussian(streams_of[3], (2 * NSTATE, LEN), 0.1, 0.6, ((1, 16),), jnp.float32),
        "a_rate": jnp.clip(jnp.exp(math.log(0.2) - 12.229789 * jax.random.uniform(streams_of[4], (NSTATE, CH), jnp.float32) ** level_of(streams_of[4], (NSTATE, CH), ((1, 16),), -0.2, 0.2)), 9.765625463842298e-07, 0.2),
        "d_skip": jnp.clip(1.0 + 0.1 * jax.random.normal(streams_of[5], (CH,), jnp.float32), 0.5, 1.5),
        "w_out": gaussian(streams_of[6], (CH, D), CH ** -0.5, 0.046875, ((0, 16), (1, 16))),
    }


def reference(u_in, z_in, delta, bc_proj, a_rate, d_skip, w_out):
    state_size = a_rate.shape[0]
    inputs_f = u_in.astype(jnp.float32)

    def advance(state, items):
        step_size, inputs_t, in_mat, out_mat = items
        state = jnp.exp(-step_size[None, :] * a_rate) * state + (step_size * inputs_t)[None, :] * in_mat[:, None]
        return state, jnp.sum(state * out_mat[:, None], axis=0)

    sequence = (delta, inputs_f, bc_proj[:state_size].T, bc_proj[state_size:].T)
    start_state = jnp.zeros((state_size, u_in.shape[1]), jnp.float32)
    _, readout = lax.scan(advance, start_state, sequence)
    mixer = readout + d_skip * inputs_f
    gated = (mixer * jax.nn.silu(z_in.astype(jnp.float32))).astype(jnp.bfloat16)
    return jnp.dot(gated, w_out, preferred_element_type=jnp.float32).astype(jnp.bfloat16)
```

```python
import functools
import math

import jax
import jax.numpy as jnp
from jax import lax
from jax.experimental import pallas as pl
from jax.experimental.pallas import tpu as pltpu
from jax.sharding import PartitionSpec as P

LANES = 128
SUB = 8
NEG_LOG2E = -math.log2(math.e)


def fill_transposed(dst, rows, groups, make):
    for g in range(groups):
        dst[pl.ds(g, rows, stride=groups), :] = make(g)


def fill_coefficients(dst, bc, rows, count):
    turned = bc.T
    for n in range(count):
        dst[pl.ds(n, rows, stride=count), :] = jnp.broadcast_to(
            turned[:, n : n + 1], (rows, LANES)
        )


def end_state_kernel(delta_ref, u_ref, bc_ref, a_ref, out_ref, d_t, w_t, b_t):
    rows, channels = delta_ref.shape
    groups = channels // LANES
    states = a_ref.shape[0] // groups

    def lanes(g):
        return slice(g * LANES, (g + 1) * LANES)

    fill_transposed(d_t, rows, groups, lambda g: delta_ref[:, lanes(g)])
    fill_transposed(
        w_t,
        rows,
        groups,
        lambda g: delta_ref[:, lanes(g)] * u_ref[:, lanes(g)].astype(jnp.float32),
    )
    fill_coefficients(b_t, bc_ref[:states, :], rows, states)
    rate = [a_ref[n * groups : (n + 1) * groups, :] * NEG_LOG2E for n in range(states)]

    def step(t, carry):
        total, state = carry
        d = d_t[pl.ds(pl.multiple_of(t * groups, groups), groups), :]
        w = w_t[pl.ds(pl.multiple_of(t * groups, groups), groups), :]
        new = []
        for n in range(states):
            b = b_t[pl.ds(t * states + n, groups, stride=0), :]
            new.append(jnp.exp2(d * rate[n]) * state[n] + w * b)
        return total + d, tuple(new)

    zero = jnp.zeros((groups, LANES), jnp.float32)
    total, state = lax.fori_loop(0, rows, step, (zero, (zero,) * states), unroll=4)
    for n in range(states):
        out_ref[n * groups : (n + 1) * groups, :] = state[n]
    out_ref[states * groups : (states + 1) * groups, :] = total


def gated_kernel(
    index_ref, delta_ref, u_ref, z_ref, bc_ref, a_ref, skip_ref, ends_ref, out_ref,
    d_t, w_t, bc_t, y_t,
):
    rows, channels = delta_ref.shape
    groups = channels // LANES
    states = a_ref.shape[0] // groups
    block = (states + 1) * groups

    def lanes(g):
        return slice(g * LANES, (g + 1) * LANES)

    fill_transposed(d_t, rows, groups, lambda g: delta_ref[:, lanes(g)])
    fill_transposed(
        w_t,
        rows,
        groups,
        lambda g: delta_ref[:, lanes(g)] * u_ref[:, lanes(g)].astype(jnp.float32),
    )
    fill_coefficients(bc_t, bc_ref[...], rows, 2 * states)
    rate = [a_ref[n * groups : (n + 1) * groups, :] * NEG_LOG2E for n in range(states)]

    def carry_in(k, state):
        base = pl.multiple_of(k * block, groups)
        total = ends_ref[pl.ds(base + states * groups, groups), :]
        return tuple(
            jnp.exp2(total * rate[n]) * state[n] + ends_ref[pl.ds(base + n * groups, groups), :]
            for n in range(states)
        )

    zero = jnp.zeros((groups, LANES), jnp.float32)
    start = lax.fori_loop(0, index_ref[0], carry_in, (zero,) * states)

    def step(t, state):
        d = d_t[pl.ds(pl.multiple_of(t * groups, groups), groups), :]
        w = w_t[pl.ds(pl.multiple_of(t * groups, groups), groups), :]
        new = []
        parts = [None] * 4
        for n in range(states):
            b = bc_t[pl.ds(t * 2 * states + n, groups, stride=0), :]
            c = bc_t[pl.ds(t * 2 * states + states + n, groups, stride=0), :]
            s = jnp.exp2(d * rate[n]) * state[n] + w * b
            new.append(s)
            term = s * c
            parts[n % 4] = term if parts[n % 4] is None else parts[n % 4] + term
        y_t[pl.ds(pl.multiple_of(t * groups, groups), groups), :] = (parts[0] + parts[1]) + (
            parts[2] + parts[3]
        )
        return tuple(new)

    lax.fori_loop(0, rows, step, start, unroll=4)

    for g in range(groups):
        y = y_t[pl.ds(g, rows, stride=groups), :]
        u = u_ref[:, lanes(g)].astype(jnp.float32)
        z = z_ref[:, lanes(g)].astype(jnp.float32)
        mixed = y + skip_ref[:, lanes(g)] * u
        out_ref[:, lanes(g)] = (mixed * (z / (1.0 + jnp.exp(-z)))).astype(jnp.bfloat16)


def whole():
    return pl.BlockSpec(memory_space=pltpu.VMEM)


def body(u_in, z_in, delta, bc_proj, a_rate, d_skip, w_out):
    rows, channels = u_in.shape
    states = a_rate.shape[0]
    groups = channels // LANES
    a_flat = a_rate.reshape(states * groups, LANES)
    flat = pltpu.VMEM((rows * groups, LANES), jnp.float32)

    ends = pl.pallas_call(
        end_state_kernel,
        out_shape=jax.ShapeDtypeStruct(((states + 1) * groups, LANES), jnp.float32),
        in_specs=[whole()] * 4,
        out_specs=whole(),
        scratch_shapes=[flat, flat, pltpu.VMEM((rows * states, LANES), jnp.float32)],
        name="end_state",
    )(delta, u_in, bc_proj, a_flat)
    all_ends = lax.all_gather(ends, "ctx", axis=0, tiled=True)
    index = lax.axis_index("ctx").astype(jnp.int32).reshape(1)
    gated = pl.pallas_call(
        gated_kernel,
        out_shape=jax.ShapeDtypeStruct((rows, channels), jnp.bfloat16),
        in_specs=[pl.BlockSpec(memory_space=pltpu.SMEM)] + [whole()] * 7,
        out_specs=whole(),
        scratch_shapes=[flat, flat, pltpu.VMEM((rows * 2 * states, LANES), jnp.float32), flat],
        name="gated",
    )(index, delta, u_in, z_in, bc_proj, a_flat, d_skip.reshape(1, channels), all_ends)

    terms = jnp.dot(
        lax.all_gather(gated, "ctx", axis=0, tiled=True), w_out, preferred_element_type=jnp.float32
    ).astype(jnp.bfloat16)
    count = lax.axis_size("exp")
    terms = terms.reshape(count, terms.shape[0] // count, terms.shape[1])
    received = lax.all_to_all(terms, "exp", split_axis=0, concat_axis=0)
    return jnp.sum(received.astype(jnp.float32), axis=0).astype(jnp.bfloat16)


def solution(mesh):
    return jax.shard_map(
        body,
        mesh=mesh,
        in_specs=(
            P("ctx", "exp"),
            P("ctx", "exp"),
            P("ctx", "exp"),
            P(None, "ctx"),
            P(None, "exp"),
            P("exp"),
            P("exp", "ctx"),
        ),
        out_specs=P("exp", "ctx"),
        check_vma=False,
    )
```

```python
import functools
import math

import jax
import jax.numpy as jnp
from jax import lax
from jax.experimental import pallas as pl
from jax.experimental.pallas import tpu as pltpu
from jax.sharding import PartitionSpec as P

LANES = 128
SUB = 8
NEG_LOG2E = -math.log2(math.e)


def fill_transposed(dst, rows, groups, make):
    for g in range(groups):
        dst[pl.ds(g, rows, stride=groups), :] = make(g)


def fill_coefficients(dst, bc, rows, count):
    turned = bc.T
    for n in range(count):
        dst[pl.ds(n, rows, stride=count), :] = jnp.broadcast_to(
            turned[:, n : n + 1], (rows, LANES)
        )


def end_state_kernel(delta_ref, u_ref, bc_ref, a_ref, out_ref, d_t, w_t, b_t):
    rows, channels = delta_ref.shape
    groups = channels // LANES
    states = a_ref.shape[0] // groups

    def lanes(g):
        return slice(g * LANES, (g + 1) * LANES)

    fill_transposed(d_t, rows, groups, lambda g: delta_ref[:, lanes(g)])
    fill_transposed(
        w_t,
        rows,
        groups,
        lambda g: delta_ref[:, lanes(g)] * u_ref[:, lanes(g)].astype(jnp.float32),
    )
    fill_coefficients(b_t, bc_ref[:states, :], rows, states)
    rate = [a_ref[n * groups : (n + 1) * groups, :] * NEG_LOG2E for n in range(states)]

    def step(t, carry):
        total, state = carry
        d = d_t[pl.ds(pl.multiple_of(t * groups, groups), groups), :]
        w = w_t[pl.ds(pl.multiple_of(t * groups, groups), groups), :]
        new = []
        for n in range(states):
            b = b_t[pl.ds(t * states + n, groups, stride=0), :]
            new.append(jnp.exp2(d * rate[n]) * state[n] + w * b)
        return total + d, tuple(new)

    zero = jnp.zeros((groups, LANES), jnp.float32)
    total, state = lax.fori_loop(0, rows, step, (zero, (zero,) * states), unroll=4)
    for n in range(states):
        out_ref[n * groups : (n + 1) * groups, :] = state[n]
    out_ref[states * groups : (states + 1) * groups, :] = total


def combine_kernel(own_ref, one_ref, two_ref, three_ref, a_ref, before_ref, through_ref):
    groups = SUB
    states = a_ref.shape[0] // groups
    last = slice(states * groups, (states + 1) * groups)
    for n in range(states):
        at = slice(n * groups, (n + 1) * groups)
        rate = a_ref[at, :] * NEG_LOG2E
        state = three_ref[at, :]
        for part in (two_ref, one_ref):
            state = jnp.exp2(part[last, :] * rate) * state + part[at, :]
        before_ref[at, :] = state
        through_ref[at, :] = jnp.exp2(own_ref[last, :] * rate) * state + own_ref[at, :]
    before = one_ref[last, :] + two_ref[last, :] + three_ref[last, :]
    before_ref[last, :] = before
    through_ref[last, :] = before + own_ref[last, :]


def gated_kernel(
    delta_ref, u_ref, z_ref, bc_ref, a_ref, skip_ref, p3_ref, p2_ref, p1_ref, p0_ref, out_ref,
    d_t, w_t, bc_t, y_t,
):
    rows, channels = delta_ref.shape
    groups = channels // LANES
    states = a_ref.shape[0] // groups

    def lanes(g):
        return slice(g * LANES, (g + 1) * LANES)

    fill_transposed(d_t, rows, groups, lambda g: delta_ref[:, lanes(g)])
    fill_transposed(
        w_t,
        rows,
        groups,
        lambda g: delta_ref[:, lanes(g)] * u_ref[:, lanes(g)].astype(jnp.float32),
    )
    fill_coefficients(bc_t, bc_ref[...], rows, 2 * states)
    rate = [a_ref[n * groups : (n + 1) * groups, :] * NEG_LOG2E for n in range(states)]

    last = slice(states * groups, (states + 1) * groups)
    start = []
    for n in range(states):
        at = slice(n * groups, (n + 1) * groups)
        state = p3_ref[at, :]
        for part in (p2_ref, p1_ref, p0_ref):
            state = jnp.exp2(part[last, :] * rate[n]) * state + part[at, :]
        start.append(state)

    def step(t, state):
        d = d_t[pl.ds(pl.multiple_of(t * groups, groups), groups), :]
        w = w_t[pl.ds(pl.multiple_of(t * groups, groups), groups), :]
        new = []
        parts = [None] * 4
        for n in range(states):
            b = bc_t[pl.ds(t * 2 * states + n, groups, stride=0), :]
            c = bc_t[pl.ds(t * 2 * states + states + n, groups, stride=0), :]
            s = jnp.exp2(d * rate[n]) * state[n] + w * b
            new.append(s)
            term = s * c
            parts[n % 4] = term if parts[n % 4] is None else parts[n % 4] + term
        y_t[pl.ds(pl.multiple_of(t * groups, groups), groups), :] = (parts[0] + parts[1]) + (
            parts[2] + parts[3]
        )
        return tuple(new)

    lax.fori_loop(0, rows, step, tuple(start), unroll=4)

    for g in range(groups):
        y = y_t[pl.ds(g, rows, stride=groups), :]
        u = u_ref[:, lanes(g)].astype(jnp.float32)
        z = z_ref[:, lanes(g)].astype(jnp.float32)
        mixed = y + skip_ref[:, lanes(g)] * u
        out_ref[:, lanes(g)] = (mixed * (z / (1.0 + jnp.exp(-z)))).astype(jnp.bfloat16)


def whole():
    return pl.BlockSpec(memory_space=pltpu.VMEM)


def project_kernel(count, place_ref, *refs):
    blocks, w_ref, outs, terms = refs[:count], refs[count], refs[count + 1 : -1], refs[-1]
    rows = blocks[0].shape[0]
    half = rows // 2
    me, x, y = place_ref[0], place_ref[1], place_ref[2]
    partner = me + 1 - 2 * lax.rem(me, 2)
    chips = count // 2
    for side, base in ((0, me), (1, partner)):
        for o in range(chips):
            k = lax.rem(base + 2 * o, count)
            at = pl.multiple_of(k * rows, rows)
            terms[pl.ds(at, rows), :] = jnp.dot(
                blocks[side * chips + o][...], w_ref[...], preferred_element_type=jnp.float32
            ).astype(jnp.bfloat16)
    for d in range(4):
        for m in range(4):
            for part, k in ((0, m * 4 + lax.rem(x + d, 4)), (1, lax.rem(y + d, 4) * 4 + m)):
                at = pl.multiple_of(k * rows + part * half, half)
                outs[part * 4 + d][m * half : (m + 1) * half, :] = terms[pl.ds(at, half), :]


def middle_kernel(place_ref, *refs):
    ins, outs, total = refs[:8], refs[8:16], refs[16]
    half = outs[0].shape[0]
    for part in range(2):
        mine = place_ref[2 - part]
        total[...] = sum(ref[...].astype(jnp.float32) for ref in ins[part * 4 : part * 4 + 4])
        for d in range(4):
            at = pl.multiple_of(lax.rem(mine + d, 4) * half, half)
            out = outs[part * 4 + d]
            out[...] = total[pl.ds(at, half), :].astype(out.dtype)


def final_kernel(*refs):
    ins, out_ref = refs[:8], refs[8]
    half = ins[0].shape[0]
    for part in range(2):
        out_ref[part * half : (part + 1) * half, :] = sum(
            ref[...].astype(jnp.float32) for ref in ins[part * 4 : part * 4 + 4]
        ).astype(out_ref.dtype)


def body(u_in, z_in, delta, bc_proj, a_rate, d_skip, w_out):
    rows, channels = u_in.shape
    states = a_rate.shape[0]
    groups = channels // LANES
    width = w_out.shape[1]
    count = lax.axis_size("ctx")
    a_flat = a_rate.reshape(states * groups, LANES)
    flat = pltpu.VMEM((rows * groups, LANES), jnp.float32)
    pair = jax.ShapeDtypeStruct(((states + 1) * groups, LANES), jnp.float32)
    smem = pl.BlockSpec(memory_space=pltpu.SMEM)
    me = lax.axis_index("ctx").astype(jnp.int32)
    spot = lax.axis_index("exp").astype(jnp.int32)
    place = jnp.stack([me, spot % 4, spot // 4])

    ends = pl.pallas_call(
        end_state_kernel,
        out_shape=pair,
        in_specs=[whole()] * 4,
        out_specs=whole(),
        scratch_shapes=[flat, flat, pltpu.VMEM((rows * states, LANES), jnp.float32)],
        name="end_state",
    )(delta, u_in, bc_proj, a_flat)

    def onward(value, shift):
        return lax.ppermute(value, "ctx", [(i, i + shift) for i in range(count - shift)])

    before, through = pl.pallas_call(
        combine_kernel,
        out_shape=(pair, pair),
        in_specs=[whole()] * 5,
        out_specs=(whole(), whole()),
        name="combine",
    )(ends, onward(ends, 1), onward(ends, 2), onward(ends, 3), a_flat)
    gated = pl.pallas_call(
        gated_kernel,
        out_shape=jax.ShapeDtypeStruct((rows, channels), jnp.bfloat16),
        in_specs=[whole()] * 10,
        out_specs=whole(),
        scratch_shapes=[flat, flat, pltpu.VMEM((rows * 2 * states, LANES), jnp.float32), flat],
        name="gated",
    )(
        delta, u_in, z_in, bc_proj, a_flat, d_skip.reshape(1, channels),
        onward(through, 12), onward(through, 8), onward(through, 4), before,
    )

    def chip_step(value, way):
        return lax.ppermute(value, "ctx", [(i, (i + 2 * way) % count) for i in range(count)])

    def swap(value):
        return lax.ppermute(value, "ctx", [(i, i ^ 1) for i in range(count)])

    chips = count // 2
    held = [None] * chips
    held[0] = gated
    for s in range(1, chips // 2 + 1):
        held[(chips - s) % chips] = chip_step(held[(chips - s + 1) % chips], 1)
        if s < chips - s:
            held[s] = chip_step(held[s - 1], -1)
    blocks = held + [swap(value) for value in held]

    half = rows // 2
    quarter = jax.ShapeDtypeStruct((4 * half, width), jnp.bfloat16)
    sent = pl.pallas_call(
        functools.partial(project_kernel, count),
        out_shape=(quarter,) * 8,
        in_specs=[smem] + [whole()] * (count + 1),
        out_specs=(whole(),) * 8,
        scratch_shapes=[pltpu.VMEM((rows * count, width), jnp.bfloat16)],
        name="project",
    )(place, *blocks, w_out)

    def across(value, dx, dy):
        pairs = [
            (y * 4 + x, (y + dy) % 4 * 4 + (x + dx) % 4) for y in range(4) for x in range(4)
        ]
        return lax.ppermute(value, "exp", pairs)

    got = [sent[0]] + [across(sent[d], d, 0) for d in range(1, 4)]
    got += [sent[4]] + [across(sent[4 + d], 0, d) for d in range(1, 4)]
    one = jax.ShapeDtypeStruct((half, width), jnp.bfloat16)
    kept = jax.ShapeDtypeStruct((half, width), jnp.float32)
    sent = pl.pallas_call(
        middle_kernel,
        out_shape=(kept, one, one, one) * 2,
        in_specs=[smem] + [whole()] * 8,
        out_specs=(whole(),) * 8,
        scratch_shapes=[pltpu.VMEM((4 * half, width), jnp.float32)],
        name="middle",
    )(place, *got)
    got = [sent[0]] + [across(sent[d], 0, d) for d in range(1, 4)]
    got += [sent[4]] + [across(sent[4 + d], d, 0) for d in range(1, 4)]
    return pl.pallas_call(
        final_kernel,
        out_shape=jax.ShapeDtypeStruct((rows, width), jnp.bfloat16),
        in_specs=[whole()] * 8,
        out_specs=whole(),
        name="final",
    )(*got)


def solution(mesh):
    return jax.shard_map(
        body,
        mesh=mesh,
        in_specs=(
            P("ctx", "exp"),
            P("ctx", "exp"),
            P("ctx", "exp"),
            P(None, "ctx"),
            P(None, "exp"),
            P("exp"),
            P("exp", "ctx"),
        ),
        out_specs=P("exp", "ctx"),
        check_vma=False,
    )
```

```python
import functools
import math

import jax
import jax.numpy as jnp
from jax import lax
from jax.experimental import pallas as pl
from jax.experimental.pallas import tpu as pltpu
from jax.sharding import PartitionSpec as P

LANES = 128
SUB = 8
NEG_LOG2E = -math.log2(math.e)


def fill_transposed(dst, rows, groups, make):
    for g in range(groups):
        dst[pl.ds(g, rows, stride=groups), :] = make(g)


def fill_coefficients(dst, bc, rows, count):
    turned = bc.T
    for n in range(count):
        dst[pl.ds(n, rows, stride=count), :] = jnp.broadcast_to(
            turned[:, n : n + 1], (rows, LANES)
        )


def end_state_kernel(delta_ref, u_ref, bc_ref, a_ref, out_ref, d_t, w_t, b_t, a_t):
    rows, channels = delta_ref.shape
    groups = channels // LANES
    states = a_ref.shape[0]

    def lanes(g):
        return slice(g * LANES, (g + 1) * LANES)

    fill_transposed(d_t, rows, groups, lambda g: delta_ref[:, lanes(g)])
    fill_transposed(
        w_t,
        rows,
        groups,
        lambda g: delta_ref[:, lanes(g)] * u_ref[:, lanes(g)].astype(jnp.float32),
    )
    fill_coefficients(b_t, bc_ref[:states, :], rows, states)
    fill_transposed(a_t, states, groups, lambda g: a_ref[:, lanes(g)])
    rate = [a_t[n * groups : (n + 1) * groups, :] * NEG_LOG2E for n in range(states)]

    def step(t, carry):
        total, state = carry
        d = d_t[pl.ds(pl.multiple_of(t * groups, groups), groups), :]
        w = w_t[pl.ds(pl.multiple_of(t * groups, groups), groups), :]
        new = []
        for n in range(states):
            b = b_t[pl.ds(t * states + n, groups, stride=0), :]
            new.append(jnp.exp2(d * rate[n]) * state[n] + w * b)
        return total + d, tuple(new)

    zero = jnp.zeros((groups, LANES), jnp.float32)
    total, state = lax.fori_loop(0, rows, step, (zero, (zero,) * states), unroll=4)
    for n in range(states):
        base = 2 * n * groups
        out_ref[base : base + groups, :] = state[n]
        out_ref[base + groups : base + 2 * groups, :] = total


def carry_kernel(me_ref, ends_ref, a_ref, out_ref, rate_t):
    count = ends_ref.shape[0] // (2 * SUB)
    fill_transposed(
        rate_t, a_ref.shape[0], SUB, lambda g: a_ref[:, g * LANES : (g + 1) * LANES] * NEG_LOG2E
    )
    rate = rate_t[pl.ds(pl.multiple_of(me_ref[0] * SUB, SUB), SUB), :]
    state = jnp.zeros((SUB, LANES), jnp.float32)
    for k in range(count):
        out_ref[k * SUB : (k + 1) * SUB, :] = state
        base = 2 * k * SUB
        total = ends_ref[base + SUB : base + 2 * SUB, :]
        state = jnp.exp2(total * rate) * state + ends_ref[base : base + SUB, :]


def gated_kernel(
    delta_ref, u_ref, z_ref, bc_ref, a_ref, skip_ref, start_ref, out_ref, d_t, w_t, bc_t, y_t, a_t,
):
    rows, channels = delta_ref.shape
    groups = channels // LANES
    states = a_ref.shape[0]

    def lanes(g):
        return slice(g * LANES, (g + 1) * LANES)

    fill_transposed(d_t, rows, groups, lambda g: delta_ref[:, lanes(g)])
    fill_transposed(
        w_t,
        rows,
        groups,
        lambda g: delta_ref[:, lanes(g)] * u_ref[:, lanes(g)].astype(jnp.float32),
    )
    fill_coefficients(bc_t, bc_ref[...], rows, 2 * states)
    fill_transposed(a_t, states, groups, lambda g: a_ref[:, lanes(g)])
    rate = [a_t[n * groups : (n + 1) * groups, :] * NEG_LOG2E for n in range(states)]

    start = [start_ref[n * groups : (n + 1) * groups, :] for n in range(states)]

    def step(t, state):
        d = d_t[pl.ds(pl.multiple_of(t * groups, groups), groups), :]
        w = w_t[pl.ds(pl.multiple_of(t * groups, groups), groups), :]
        new = []
        parts = [None] * 4
        for n in range(states):
            b = bc_t[pl.ds(t * 2 * states + n, groups, stride=0), :]
            c = bc_t[pl.ds(t * 2 * states + states + n, groups, stride=0), :]
            s = jnp.exp2(d * rate[n]) * state[n] + w * b
            new.append(s)
            term = s * c
            parts[n % 4] = term if parts[n % 4] is None else parts[n % 4] + term
        y_t[pl.ds(pl.multiple_of(t * groups, groups), groups), :] = (parts[0] + parts[1]) + (
            parts[2] + parts[3]
        )
        return tuple(new)

    lax.fori_loop(0, rows, step, tuple(start), unroll=4)

    for g in range(groups):
        y = y_t[pl.ds(g, rows, stride=groups), :]
        u = u_ref[:, lanes(g)].astype(jnp.float32)
        z = z_ref[:, lanes(g)].astype(jnp.float32)
        mixed = y + skip_ref[:, lanes(g)] * u
        out_ref[:, lanes(g)] = (mixed * (z / (1.0 + jnp.exp(-z)))).astype(jnp.bfloat16)


def project_kernel(count, me_ref, *refs):
    blocks, w_ref, out_ref = refs[:count], refs[count], refs[count + 1]
    rows = blocks[0].shape[0]
    me = me_ref[0]
    core = lax.rem(me, 2)
    chip = me - core
    way = 2 - 4 * core
    units = (count - 2) // 2
    homes = [chip + core, chip + 1 - core]
    for side in (-1, 1):
        for unit in range(units):
            same = (unit % 2 == 0) == (side == -1)
            parity = core if same else 1 - core
            homes.append(chip + side * way * (unit // 2 + 1) + parity)
    for block, home in zip(blocks, homes):
        at = pl.multiple_of(lax.rem(home + 2 * count, count) * rows, rows)
        out_ref[pl.ds(at, rows), :] = jnp.dot(
            block[...], w_ref[...], preferred_element_type=jnp.float32
        ).astype(jnp.bfloat16)


def whole():
    return pl.BlockSpec(memory_space=pltpu.VMEM)


def body(u_in, z_in, delta, bc_proj, a_rate, d_skip, w_out):
    rows, channels = u_in.shape
    states = a_rate.shape[0]
    groups = channels // LANES
    width = w_out.shape[1]
    count = lax.axis_size("ctx")
    flat = pltpu.VMEM((rows * groups, LANES), jnp.float32)
    rates = pltpu.VMEM((states * groups, LANES), jnp.float32)
    smem = pl.BlockSpec(memory_space=pltpu.SMEM)
    me = lax.axis_index("ctx").astype(jnp.int32).reshape(1)

    ends = pl.pallas_call(
        end_state_kernel,
        out_shape=jax.ShapeDtypeStruct((2 * states * groups, LANES), jnp.float32),
        in_specs=[whole()] * 4,
        out_specs=whole(),
        scratch_shapes=[flat, flat, pltpu.VMEM((rows * states, LANES), jnp.float32), rates],
        name="end_state",
    )(delta, u_in, bc_proj, a_rate)
    ends = lax.all_to_all(ends, "ctx", split_axis=0, concat_axis=0, tiled=True)
    entering = pl.pallas_call(
        carry_kernel,
        out_shape=jax.ShapeDtypeStruct((count * groups, LANES), jnp.float32),
        in_specs=[smem, whole(), whole()],
        out_specs=whole(),
        scratch_shapes=[rates],
        name="carry",
    )(me, ends, a_rate)
    entering = lax.all_to_all(entering, "ctx", split_axis=0, concat_axis=0, tiled=True)
    gated = pl.pallas_call(
        gated_kernel,
        out_shape=jax.ShapeDtypeStruct((rows, channels), jnp.bfloat16),
        in_specs=[whole()] * 7,
        out_specs=whole(),
        scratch_shapes=[
            flat, flat, pltpu.VMEM((rows * 2 * states, LANES), jnp.float32), flat, rates
        ],
        name="gated",
    )(delta, u_in, z_in, bc_proj, a_rate, d_skip.reshape(1, channels), entering)

    ring = [(i, (i + 2 - 4 * (i % 2)) % count) for i in range(count)]
    trade = [(i, i ^ 1) for i in range(count)]
    local = [gated, lax.ppermute(gated, "ctx", trade)]
    arrived = []
    for unit in range(count // 2 - 1):
        source = (local + arrived)[unit]
        arrived.append(lax.ppermute(source, "ctx", ring))
    traded = [lax.ppermute(value, "ctx", trade) for value in arrived]
    terms = pl.pallas_call(
        functools.partial(project_kernel, count),
        out_shape=jax.ShapeDtypeStruct((rows * count, width), jnp.bfloat16),
        in_specs=[smem] + [whole()] * (count + 1),
        out_specs=whole(),
        name="project",
    )(me, *local, *arrived, *traded, w_out)

    received = lax.all_to_all(
        terms.reshape(count, rows, width), "exp", split_axis=0, concat_axis=0
    )
    return jnp.sum(received.astype(jnp.float32), axis=0).astype(jnp.bfloat16)


def solution(mesh):
    return jax.shard_map(
        body,
        mesh=mesh,
        in_specs=(
            P("ctx", "exp"),
            P("ctx", "exp"),
            P("ctx", "exp"),
            P(None, "ctx"),
            P(None, "exp"),
            P("exp"),
            P("exp", "ctx"),
        ),
        out_specs=P("exp", "ctx"),
        check_vma=False,
    )
```

```python
import functools
import math

import jax
import jax.numpy as jnp
from jax import lax
from jax.experimental import pallas as pl
from jax.experimental.pallas import tpu as pltpu
from jax.sharding import PartitionSpec as P

LANES = 128
SUB = 8
NEG_LOG2E = -math.log2(math.e)


def fill_transposed(dst, rows, groups, make):
    for g in range(groups):
        dst[pl.ds(g, rows, stride=groups), :] = make(g)


def fill_coefficients(dst, bc, rows, count):
    turned = bc.T
    for n in range(count):
        dst[pl.ds(n, rows, stride=count), :] = jnp.broadcast_to(
            turned[:, n : n + 1], (rows, LANES)
        )


def end_state_kernel(delta_ref, u_ref, bc_ref, a_ref, out_ref, d_t, w_t, b_t, a_t):
    rows, channels = delta_ref.shape
    groups = channels // LANES
    states = a_ref.shape[0]

    def lanes(g):
        return slice(g * LANES, (g + 1) * LANES)

    fill_transposed(d_t, rows, groups, lambda g: delta_ref[:, lanes(g)])
    fill_transposed(
        w_t,
        rows,
        groups,
        lambda g: delta_ref[:, lanes(g)] * u_ref[:, lanes(g)].astype(jnp.float32),
    )
    fill_coefficients(b_t, bc_ref[:states, :], rows, states)
    fill_transposed(a_t, states, groups, lambda g: a_ref[:, lanes(g)])
    rate = [a_t[n * groups : (n + 1) * groups, :] * NEG_LOG2E for n in range(states)]

    def step(t, carry):
        total, state = carry
        d = d_t[pl.ds(pl.multiple_of(t * groups, groups), groups), :]
        w = w_t[pl.ds(pl.multiple_of(t * groups, groups), groups), :]
        new = []
        for n in range(states):
            b = b_t[pl.ds(t * states + n, groups, stride=0), :]
            new.append(jnp.exp2(d * rate[n]) * state[n] + w * b)
        return total + d, tuple(new)

    zero = jnp.zeros((groups, LANES), jnp.float32)
    total, state = lax.fori_loop(0, rows, step, (zero, (zero,) * states), unroll=4)
    for n in range(states):
        base = 2 * n * groups
        out_ref[base : base + groups, :] = state[n]
        out_ref[base + groups : base + 2 * groups, :] = total


def carry_kernel(me_ref, ends_ref, a_ref, out_ref, rate_t):
    count = ends_ref.shape[0] // (2 * SUB)
    fill_transposed(
        rate_t, a_ref.shape[0], SUB, lambda g: a_ref[:, g * LANES : (g + 1) * LANES] * NEG_LOG2E
    )
    rate = rate_t[pl.ds(pl.multiple_of(me_ref[0] * SUB, SUB), SUB), :]
    state = jnp.zeros((SUB, LANES), jnp.float32)
    for k in range(count):
        out_ref[k * SUB : (k + 1) * SUB, :] = state
        base = 2 * k * SUB
        total = ends_ref[base + SUB : base + 2 * SUB, :]
        state = jnp.exp2(total * rate) * state + ends_ref[base : base + SUB, :]


def gated_kernel(
    delta_ref, u_ref, z_ref, bc_ref, a_ref, skip_ref, start_ref, top_ref, low_ref,
    d_t, w_t, bc_t, y_t, a_t,
):
    rows, channels = delta_ref.shape
    groups = channels // LANES
    states = a_ref.shape[0]

    def lanes(g):
        return slice(g * LANES, (g + 1) * LANES)

    fill_transposed(d_t, rows, groups, lambda g: delta_ref[:, lanes(g)])
    fill_transposed(
        w_t,
        rows,
        groups,
        lambda g: delta_ref[:, lanes(g)] * u_ref[:, lanes(g)].astype(jnp.float32),
    )
    fill_coefficients(bc_t, bc_ref[...], rows, 2 * states)
    fill_transposed(a_t, states, groups, lambda g: a_ref[:, lanes(g)])
    rate = [a_t[n * groups : (n + 1) * groups, :] * NEG_LOG2E for n in range(states)]

    start = [start_ref[n * groups : (n + 1) * groups, :] for n in range(states)]

    def step(t, state):
        d = d_t[pl.ds(pl.multiple_of(t * groups, groups), groups), :]
        w = w_t[pl.ds(pl.multiple_of(t * groups, groups), groups), :]
        new = []
        parts = [None] * 4
        for n in range(states):
            b = bc_t[pl.ds(t * 2 * states + n, groups, stride=0), :]
            c = bc_t[pl.ds(t * 2 * states + states + n, groups, stride=0), :]
            s = jnp.exp2(d * rate[n]) * state[n] + w * b
            new.append(s)
            term = s * c
            parts[n % 4] = term if parts[n % 4] is None else parts[n % 4] + term
        y_t[pl.ds(pl.multiple_of(t * groups, groups), groups), :] = (parts[0] + parts[1]) + (
            parts[2] + parts[3]
        )
        return tuple(new)

    lax.fori_loop(0, rows, step, tuple(start), unroll=4)

    for g in range(groups):
        y = y_t[pl.ds(g, rows, stride=groups), :]
        u = u_ref[:, lanes(g)].astype(jnp.float32)
        z = z_ref[:, lanes(g)].astype(jnp.float32)
        mixed = y + skip_ref[:, lanes(g)] * u
        gated = (mixed * (z / (1.0 + jnp.exp(-z)))).astype(jnp.bfloat16)
        top_ref[:, lanes(g)] = gated[: rows // 2]
        low_ref[:, lanes(g)] = gated[rows // 2 :]


def project_kernel(places, me_ref, w_ref, *refs):
    units = len(places)
    blocks, out_ref, joined, result, sems = refs[:units], *refs[-4:]
    rows = blocks[0].shape[0]
    count = out_ref.shape[0] // (2 * rows)
    me = me_ref[0]
    partner = me + 1 - 2 * lax.rem(me, 2)
    for i, block in enumerate(blocks):
        joined[i * rows : (i + 1) * rows, :] = block[...]
    result[...] = jnp.dot(
        joined[...], w_ref[...], preferred_element_type=jnp.float32
    ).astype(jnp.bfloat16)
    copies = []
    for i, (side, offset, half) in enumerate(places):
        home = lax.rem((partner if side else me) + 2 * offset, count)
        at = pl.multiple_of((2 * home + half) * rows, rows)
        copies.append(
            pltpu.make_async_copy(
                result.at[pl.ds(i * rows, rows), :], out_ref.at[pl.ds(at, rows), :], sems.at[i]
            )
        )
        copies[-1].start()
    for copy in copies:
        copy.wait()


def whole():
    return pl.BlockSpec(memory_space=pltpu.VMEM)


def body(u_in, z_in, delta, bc_proj, a_rate, d_skip, w_out):
    rows, channels = u_in.shape
    states = a_rate.shape[0]
    groups = channels // LANES
    width = w_out.shape[1]
    count = lax.axis_size("ctx")
    flat = pltpu.VMEM((rows * groups, LANES), jnp.float32)
    rates = pltpu.VMEM((states * groups, LANES), jnp.float32)
    smem = pl.BlockSpec(memory_space=pltpu.SMEM)
    me = lax.axis_index("ctx").astype(jnp.int32).reshape(1)

    ends = pl.pallas_call(
        end_state_kernel,
        out_shape=jax.ShapeDtypeStruct((2 * states * groups, LANES), jnp.float32),
        in_specs=[whole()] * 4,
        out_specs=whole(),
        scratch_shapes=[flat, flat, pltpu.VMEM((rows * states, LANES), jnp.float32), rates],
        name="end_state",
    )(delta, u_in, bc_proj, a_rate)
    ends = lax.all_to_all(ends, "ctx", split_axis=0, concat_axis=0, tiled=True)
    entering = pl.pallas_call(
        carry_kernel,
        out_shape=jax.ShapeDtypeStruct((count * groups, LANES), jnp.float32),
        in_specs=[smem, whole(), whole()],
        out_specs=whole(),
        scratch_shapes=[rates],
        name="carry",
    )(me, ends, a_rate)
    entering = lax.all_to_all(entering, "ctx", split_axis=0, concat_axis=0, tiled=True)
    half_block = jax.ShapeDtypeStruct((rows // 2, channels), jnp.bfloat16)
    halves = pl.pallas_call(
        gated_kernel,
        out_shape=(half_block, half_block),
        in_specs=[whole()] * 7,
        out_specs=(whole(), whole()),
        scratch_shapes=[
            flat, flat, pltpu.VMEM((rows * 2 * states, LANES), jnp.float32), flat, rates
        ],
        name="gated",
    )(delta, u_in, z_in, bc_proj, a_rate, d_skip.reshape(1, channels), entering)

    up = [(i, (i + 2) % count) for i in range(count)]
    down = [(i, (i - 2) % count) for i in range(count)]
    trade = [(i, i ^ 1) for i in range(count)]
    chips = count // 2
    held = {(0, h): value for h, value in enumerate(halves)}
    for s in range(1, chips // 2 + 1):
        for h in range(2):
            if s < chips - s or h == 0:
                held[chips - s, h] = lax.ppermute(held[(chips - s + 1) % chips, h], "ctx", up)
            if s < chips - s or h == 1:
                held[s, h] = lax.ppermute(held[s - 1, h], "ctx", down)
    late = range(chips // 2 - 1, chips // 2 + 2)
    terms = None
    for now in (False, True):
        keys = [key for key in held if (key[0] in late) == now]
        places = [(0, *key) for key in keys] + [(1, *key) for key in keys]
        blocks = [held[key] for key in keys]
        blocks += [lax.ppermute(value, "ctx", trade) for value in blocks]
        done = [] if terms is None else [terms]
        tall = len(places) * (rows // 2)
        terms = pl.pallas_call(
            functools.partial(project_kernel, tuple(places)),
            out_shape=jax.ShapeDtypeStruct((rows * count, width), jnp.bfloat16),
            in_specs=[smem]
            + [whole()] * (len(places) + 1)
            + [pl.BlockSpec(memory_space=pl.ANY)] * len(done),
            out_specs=pl.BlockSpec(memory_space=pl.ANY),
            scratch_shapes=[
                pltpu.VMEM((tall, channels), jnp.bfloat16),
                pltpu.VMEM((tall, width), jnp.bfloat16),
                pltpu.SemaphoreType.DMA((len(places),)),
            ],
            input_output_aliases={len(places) + 2: 0} if done else {},
            cost_estimate=pl.CostEstimate(
                flops=2 * tall * channels * width,
                bytes_accessed=2 * tall * (channels + width),
                transcendentals=0,
            ),
            name="project",
        )(me, w_out, *blocks, *done)

    received = lax.all_to_all(
        terms.reshape(count, rows, width), "exp", split_axis=0, concat_axis=0
    )
    return jnp.sum(received.astype(jnp.float32), axis=0).astype(jnp.bfloat16)


def solution(mesh):
    return jax.shard_map(
        body,
        mesh=mesh,
        in_specs=(
            P("ctx", "exp"),
            P("ctx", "exp"),
            P("ctx", "exp"),
            P(None, "ctx"),
            P(None, "exp"),
            P("exp"),
            P("exp", "ctx"),
        ),
        out_specs=P("exp", "ctx"),
        check_vma=False,
    )
```

```python
import functools
import math

import jax
import jax.numpy as jnp
from jax import lax
from jax.experimental import pallas as pl
from jax.experimental.pallas import tpu as pltpu
from jax.sharding import PartitionSpec as P

LANES = 128
SUB = 8
NEG_LOG2E = -math.log2(math.e)


def fill_transposed(dst, rows, groups, make):
    for g in range(groups):
        dst[pl.ds(g, rows, stride=groups), :] = make(g)


def fill_coefficients(dst, bc, rows, count):
    turned = bc.T
    for n in range(count):
        dst[pl.ds(n, rows, stride=count), :] = jnp.broadcast_to(
            turned[:, n : n + 1], (rows, LANES)
        )


def end_state_kernel(delta_ref, u_ref, bc_ref, a_ref, out_ref, d_t, w_t, b_t, a_t):
    rows, channels = delta_ref.shape
    groups = channels // LANES
    states = a_ref.shape[0]

    def lanes(g):
        return slice(g * LANES, (g + 1) * LANES)

    fill_transposed(d_t, rows, groups, lambda g: delta_ref[:, lanes(g)])
    fill_transposed(
        w_t,
        rows,
        groups,
        lambda g: delta_ref[:, lanes(g)] * u_ref[:, lanes(g)].astype(jnp.float32),
    )
    fill_coefficients(b_t, bc_ref[:states, :], rows, states)
    fill_transposed(a_t, states, groups, lambda g: a_ref[:, lanes(g)])
    rate = [a_t[n * groups : (n + 1) * groups, :] * NEG_LOG2E for n in range(states)]

    def step(t, carry):
        total, state = carry
        d = d_t[pl.ds(pl.multiple_of(t * groups, groups), groups), :]
        w = w_t[pl.ds(pl.multiple_of(t * groups, groups), groups), :]
        new = []
        for n in range(states):
            b = b_t[pl.ds(t * states + n, groups, stride=0), :]
            new.append(jnp.exp2(d * rate[n]) * state[n] + w * b)
        return total + d, tuple(new)

    zero = jnp.zeros((groups, LANES), jnp.float32)
    total, state = lax.fori_loop(0, rows, step, (zero, (zero,) * states), unroll=4)
    for n in range(states):
        base = 2 * n * groups
        out_ref[base : base + groups, :] = state[n]
        out_ref[base + groups : base + 2 * groups, :] = total


def carry_kernel(me_ref, ends_ref, a_ref, out_ref, rate_t):
    count = ends_ref.shape[0] // (2 * SUB)
    fill_transposed(
        rate_t, a_ref.shape[0], SUB, lambda g: a_ref[:, g * LANES : (g + 1) * LANES] * NEG_LOG2E
    )
    rate = rate_t[pl.ds(pl.multiple_of(me_ref[0] * SUB, SUB), SUB), :]
    state = jnp.zeros((SUB, LANES), jnp.float32)
    for k in range(count):
        out_ref[k * SUB : (k + 1) * SUB, :] = state
        base = 2 * k * SUB
        total = ends_ref[base + SUB : base + 2 * SUB, :]
        state = jnp.exp2(total * rate) * state + ends_ref[base : base + SUB, :]


def local_kernel(delta_ref, u_ref, bc_ref, a_ref, y_ref, sum_ref, c_ref, d_t, w_t, b_t, a_t):
    rows, channels = delta_ref.shape
    groups = channels // LANES
    states = a_ref.shape[0]

    def lanes(g):
        return slice(g * LANES, (g + 1) * LANES)

    fill_transposed(d_t, rows, groups, lambda g: delta_ref[:, lanes(g)])
    fill_transposed(
        w_t,
        rows,
        groups,
        lambda g: delta_ref[:, lanes(g)] * u_ref[:, lanes(g)].astype(jnp.float32),
    )
    fill_coefficients(b_t, bc_ref[:states, :], rows, states)
    fill_coefficients(c_ref, bc_ref[states:, :], rows, states)
    fill_transposed(a_t, states, groups, lambda g: a_ref[:, lanes(g)])
    rate = [a_t[n * groups : (n + 1) * groups, :] * NEG_LOG2E for n in range(states)]

    def step(t, carry):
        total, state = carry
        at = pl.ds(pl.multiple_of(t * groups, groups), groups)
        d = d_t[at, :]
        w = w_t[at, :]
        new = []
        parts = [None] * 4
        for n in range(states):
            b = b_t[pl.ds(t * states + n, groups, stride=0), :]
            c = c_ref[pl.ds(t * states + n, groups, stride=0), :]
            s = jnp.exp2(d * rate[n]) * state[n] + w * b
            new.append(s)
            term = s * c
            parts[n % 4] = term if parts[n % 4] is None else parts[n % 4] + term
        y_ref[at, :] = (parts[0] + parts[1]) + (parts[2] + parts[3])
        total = total + d
        sum_ref[at, :] = total
        return total, tuple(new)

    zero = jnp.zeros((groups, LANES), jnp.float32)
    lax.fori_loop(0, rows, step, (zero, (zero,) * states), unroll=4)


def gated_kernel(
    u_ref, z_ref, a_ref, skip_ref, start_ref, y_ref, sum_ref, c_ref, out_ref, y_t, a_t
):
    rows, channels = u_ref.shape
    groups = channels // LANES
    states = a_ref.shape[0]

    def lanes(g):
        return slice(g * LANES, (g + 1) * LANES)

    fill_transposed(a_t, states, groups, lambda g: a_ref[:, lanes(g)])
    rate = [a_t[n * groups : (n + 1) * groups, :] * NEG_LOG2E for n in range(states)]
    start = [start_ref[n * groups : (n + 1) * groups, :] for n in range(states)]

    def step(t, carry):
        at = pl.ds(pl.multiple_of(t * groups, groups), groups)
        total = sum_ref[at, :]
        parts = [None] * 4
        for n in range(states):
            c = c_ref[pl.ds(t * states + n, groups, stride=0), :]
            term = jnp.exp2(total * rate[n]) * start[n] * c
            parts[n % 4] = term if parts[n % 4] is None else parts[n % 4] + term
        y_t[at, :] = y_ref[at, :] + ((parts[0] + parts[1]) + (parts[2] + parts[3]))
        return carry

    lax.fori_loop(0, rows, step, 0, unroll=4)

    for g in range(groups):
        y = y_t[pl.ds(g, rows, stride=groups), :]
        u = u_ref[:, lanes(g)].astype(jnp.float32)
        z = z_ref[:, lanes(g)].astype(jnp.float32)
        mixed = y + skip_ref[:, lanes(g)] * u
        out_ref[:, lanes(g)] = (mixed * (z / (1.0 + jnp.exp(-z)))).astype(jnp.bfloat16)


def project_kernel(count, me_ref, *refs):
    blocks, w_ref, out_ref = refs[:count], refs[count], refs[count + 1]
    rows = blocks[0].shape[0]
    me = me_ref[0]
    core = lax.rem(me, 2)
    chip = me - core
    way = 2 - 4 * core
    units = (count - 2) // 2
    homes = [chip + core, chip + 1 - core]
    for side in (-1, 1):
        for unit in range(units):
            same = (unit % 2 == 0) == (side == -1)
            parity = core if same else 1 - core
            homes.append(chip + side * way * (unit // 2 + 1) + parity)
    for block, home in zip(blocks, homes):
        at = pl.multiple_of(lax.rem(home + 2 * count, count) * rows, rows)
        out_ref[pl.ds(at, rows), :] = jnp.dot(
            block[...], w_ref[...], preferred_element_type=jnp.float32
        ).astype(jnp.bfloat16)


def whole():
    return pl.BlockSpec(memory_space=pltpu.VMEM)


def body(u_in, z_in, delta, bc_proj, a_rate, d_skip, w_out):
    rows, channels = u_in.shape
    states = a_rate.shape[0]
    groups = channels // LANES
    width = w_out.shape[1]
    count = lax.axis_size("ctx")
    flat = pltpu.VMEM((rows * groups, LANES), jnp.float32)
    rates = pltpu.VMEM((states * groups, LANES), jnp.float32)
    smem = pl.BlockSpec(memory_space=pltpu.SMEM)
    me = lax.axis_index("ctx").astype(jnp.int32).reshape(1)

    ends = pl.pallas_call(
        end_state_kernel,
        out_shape=jax.ShapeDtypeStruct((2 * states * groups, LANES), jnp.float32),
        in_specs=[whole()] * 4,
        out_specs=whole(),
        scratch_shapes=[flat, flat, pltpu.VMEM((rows * states, LANES), jnp.float32), rates],
        name="end_state",
    )(delta, u_in, bc_proj, a_rate)
    tokens = jax.ShapeDtypeStruct((rows * groups, LANES), jnp.float32)
    spread = pltpu.VMEM((rows * states, LANES), jnp.float32)
    local = pl.pallas_call(
        local_kernel,
        out_shape=(tokens, tokens, jax.ShapeDtypeStruct((rows * states, LANES), jnp.float32)),
        in_specs=[whole()] * 4,
        out_specs=(whole(),) * 3,
        scratch_shapes=[flat, flat, spread, rates],
        cost_estimate=pl.CostEstimate(
            flops=6 * rows * channels * states,
            bytes_accessed=4 * rows * (4 * channels + states * LANES),
            transcendentals=rows * channels * states,
        ),
        name="local",
    )(delta, u_in, bc_proj, a_rate)
    ends = lax.all_to_all(ends, "ctx", split_axis=0, concat_axis=0, tiled=True)
    entering = pl.pallas_call(
        carry_kernel,
        out_shape=jax.ShapeDtypeStruct((count * groups, LANES), jnp.float32),
        in_specs=[smem, whole(), whole()],
        out_specs=whole(),
        scratch_shapes=[rates],
        name="carry",
    )(me, ends, a_rate)
    entering = lax.all_to_all(entering, "ctx", split_axis=0, concat_axis=0, tiled=True)
    gated = pl.pallas_call(
        gated_kernel,
        out_shape=jax.ShapeDtypeStruct((rows, channels), jnp.bfloat16),
        in_specs=[whole()] * 8,
        out_specs=whole(),
        scratch_shapes=[flat, rates],
        name="gated",
    )(u_in, z_in, a_rate, d_skip.reshape(1, channels), entering, *local)

    ring = [(i, (i + 2 - 4 * (i % 2)) % count) for i in range(count)]
    trade = [(i, i ^ 1) for i in range(count)]
    chip_blocks = [gated, lax.ppermute(gated, "ctx", trade)]
    arrived = []
    for unit in range(count // 2 - 1):
        source = (chip_blocks + arrived)[unit]
        arrived.append(lax.ppermute(source, "ctx", ring))
    traded = [lax.ppermute(value, "ctx", trade) for value in arrived]
    terms = pl.pallas_call(
        functools.partial(project_kernel, count),
        out_shape=jax.ShapeDtypeStruct((rows * count, width), jnp.bfloat16),
        in_specs=[smem] + [whole()] * (count + 1),
        out_specs=whole(),
        name="project",
    )(me, *chip_blocks, *arrived, *traded, w_out)

    received = lax.all_to_all(
        terms.reshape(count, rows, width), "exp", split_axis=0, concat_axis=0
    )
    return jnp.sum(received.astype(jnp.float32), axis=0).astype(jnp.bfloat16)


def solution(mesh):
    return jax.shard_map(
        body,
        mesh=mesh,
        in_specs=(
            P("ctx", "exp"),
            P("ctx", "exp"),
            P("ctx", "exp"),
            P(None, "ctx"),
            P(None, "exp"),
            P("exp"),
            P("exp", "ctx"),
        ),
        out_specs=P("exp", "ctx"),
        check_vma=False,
    )
```

```python
import functools
import math

import jax
import jax.numpy as jnp
from jax import lax
from jax.experimental import pallas as pl
from jax.experimental.pallas import tpu as pltpu
from jax.sharding import PartitionSpec as P

LANES = 128
SUB = 8
NEG_LOG2E = -math.log2(math.e)


def fill_transposed(dst, rows, groups, make):
    for g in range(groups):
        dst[pl.ds(g, rows, stride=groups), :] = make(g)


def fill_coefficients(dst, bc, rows, count):
    turned = bc.T
    for n in range(count):
        dst[pl.ds(n, rows, stride=count), :] = jnp.broadcast_to(
            turned[:, n : n + 1], (rows, LANES)
        )


def end_state_kernel(delta_ref, u_ref, bc_ref, a_ref, out_ref, d_t, w_t, b_t, a_t):
    rows, channels = delta_ref.shape
    groups = channels // LANES
    states = a_ref.shape[0]

    def lanes(g):
        return slice(g * LANES, (g + 1) * LANES)

    fill_transposed(d_t, rows, groups, lambda g: delta_ref[:, lanes(g)])
    fill_transposed(
        w_t,
        rows,
        groups,
        lambda g: delta_ref[:, lanes(g)] * u_ref[:, lanes(g)].astype(jnp.float32),
    )
    fill_coefficients(b_t, bc_ref[:states, :], rows, states)
    fill_transposed(a_t, states, groups, lambda g: a_ref[:, lanes(g)])
    rate = [a_t[n * groups : (n + 1) * groups, :] * NEG_LOG2E for n in range(states)]

    def step(t, carry):
        total, state = carry
        d = d_t[pl.ds(pl.multiple_of(t * groups, groups), groups), :]
        w = w_t[pl.ds(pl.multiple_of(t * groups, groups), groups), :]
        new = []
        for n in range(states):
            b = b_t[pl.ds(t * states + n, groups, stride=0), :]
            new.append(jnp.exp2(d * rate[n]) * state[n] + w * b)
        return total + d, tuple(new)

    zero = jnp.zeros((groups, LANES), jnp.float32)
    total, state = lax.fori_loop(0, rows, step, (zero, (zero,) * states), unroll=4)
    for n in range(states):
        base = 2 * n * groups
        out_ref[base : base + groups, :] = state[n]
        out_ref[base + groups : base + 2 * groups, :] = total


def carry_kernel(me_ref, ends_ref, a_ref, out_ref, rate_t):
    count = ends_ref.shape[0] // (2 * SUB)
    fill_transposed(
        rate_t, a_ref.shape[0], SUB, lambda g: a_ref[:, g * LANES : (g + 1) * LANES] * NEG_LOG2E
    )
    rate = rate_t[pl.ds(pl.multiple_of(me_ref[0] * SUB, SUB), SUB), :]
    state = jnp.zeros((SUB, LANES), jnp.float32)
    for k in range(count):
        out_ref[k * SUB : (k + 1) * SUB, :] = state
        base = 2 * k * SUB
        total = ends_ref[base + SUB : base + 2 * SUB, :]
        state = jnp.exp2(total * rate) * state + ends_ref[base : base + SUB, :]


def local_kernel(delta_ref, u_ref, bc_ref, a_ref, y_ref, sum_ref, c_ref, d_t, w_t, b_t, a_t):
    rows, channels = delta_ref.shape
    groups = channels // LANES
    states = a_ref.shape[0]

    def lanes(g):
        return slice(g * LANES, (g + 1) * LANES)

    fill_transposed(d_t, rows, groups, lambda g: delta_ref[:, lanes(g)])
    fill_transposed(
        w_t,
        rows,
        groups,
        lambda g: delta_ref[:, lanes(g)] * u_ref[:, lanes(g)].astype(jnp.float32),
    )
    fill_coefficients(b_t, bc_ref[:states, :], rows, states)
    fill_coefficients(c_ref, bc_ref[states:, :], rows, states)
    fill_transposed(a_t, states, groups, lambda g: a_ref[:, lanes(g)])
    rate = [a_t[n * groups : (n + 1) * groups, :] * NEG_LOG2E for n in range(states)]

    def step(t, carry):
        total, state = carry
        at = pl.ds(pl.multiple_of(t * groups, groups), groups)
        d = d_t[at, :]
        w = w_t[at, :]
        new = []
        parts = [None] * 4
        for n in range(states):
            b = b_t[pl.ds(t * states + n, groups, stride=0), :]
            c = c_ref[pl.ds(t * states + n, groups, stride=0), :]
            s = jnp.exp2(d * rate[n]) * state[n] + w * b
            new.append(s)
            term = s * c
            parts[n % 4] = term if parts[n % 4] is None else parts[n % 4] + term
        y_ref[at, :] = (parts[0] + parts[1]) + (parts[2] + parts[3])
        total = total + d
        sum_ref[at, :] = total
        return total, tuple(new)

    zero = jnp.zeros((groups, LANES), jnp.float32)
    lax.fori_loop(0, rows, step, (zero, (zero,) * states), unroll=4)


def gated_kernel(
    u_ref, z_ref, a_ref, skip_ref, start_ref, y_ref, sum_ref, c_ref, out_ref, y_t, a_t
):
    rows, channels = u_ref.shape
    groups = channels // LANES
    states = a_ref.shape[0]

    def lanes(g):
        return slice(g * LANES, (g + 1) * LANES)

    fill_transposed(a_t, states, groups, lambda g: a_ref[:, lanes(g)])
    rate = [a_t[n * groups : (n + 1) * groups, :] * NEG_LOG2E for n in range(states)]
    start = [start_ref[n * groups : (n + 1) * groups, :] for n in range(states)]

    def step(t, carry):
        at = pl.ds(pl.multiple_of(t * groups, groups), groups)
        total = sum_ref[at, :]
        parts = [None] * 4
        for n in range(states):
            c = c_ref[pl.ds(t * states + n, groups, stride=0), :]
            term = jnp.exp2(total * rate[n]) * start[n] * c
            parts[n % 4] = term if parts[n % 4] is None else parts[n % 4] + term
        y_t[at, :] = y_ref[at, :] + ((parts[0] + parts[1]) + (parts[2] + parts[3]))
        return carry

    lax.fori_loop(0, rows, step, 0, unroll=4)

    for g in range(groups):
        y = y_t[pl.ds(g, rows, stride=groups), :]
        u = u_ref[:, lanes(g)].astype(jnp.float32)
        z = z_ref[:, lanes(g)].astype(jnp.float32)
        mixed = y + skip_ref[:, lanes(g)] * u
        out_ref[:, lanes(g)] = (mixed * (z / (1.0 + jnp.exp(-z)))).astype(jnp.bfloat16)


def project_kernel(places, me_ref, w_ref, *refs):
    units = len(places)
    blocks, out_ref, joined, result, sems = refs[:units], *refs[-4:]
    rows = blocks[0].shape[0]
    count = out_ref.shape[0] // rows
    me = me_ref[0]
    core = lax.rem(me, 2)
    way = 2 - 4 * core
    for i, block in enumerate(blocks):
        joined[i * rows : (i + 1) * rows, :] = block[...]
    result[...] = jnp.dot(
        joined[...], w_ref[...], preferred_element_type=jnp.float32
    ).astype(jnp.bfloat16)
    copies = []
    for i, (step, same) in enumerate(places):
        home = me - core + step * way + (core if same else 1 - core)
        at = pl.multiple_of(lax.rem(home + 2 * count, count) * rows, rows)
        copies.append(
            pltpu.make_async_copy(
                result.at[pl.ds(i * rows, rows), :], out_ref.at[pl.ds(at, rows), :], sems.at[i]
            )
        )
        copies[-1].start()
    for copy in copies:
        copy.wait()


def whole():
    return pl.BlockSpec(memory_space=pltpu.VMEM)


def body(u_in, z_in, delta, bc_proj, a_rate, d_skip, w_out):
    rows, channels = u_in.shape
    states = a_rate.shape[0]
    groups = channels // LANES
    width = w_out.shape[1]
    count = lax.axis_size("ctx")
    flat = pltpu.VMEM((rows * groups, LANES), jnp.float32)
    rates = pltpu.VMEM((states * groups, LANES), jnp.float32)
    smem = pl.BlockSpec(memory_space=pltpu.SMEM)
    me = lax.axis_index("ctx").astype(jnp.int32).reshape(1)

    ends = pl.pallas_call(
        end_state_kernel,
        out_shape=jax.ShapeDtypeStruct((2 * states * groups, LANES), jnp.float32),
        in_specs=[whole()] * 4,
        out_specs=whole(),
        scratch_shapes=[flat, flat, pltpu.VMEM((rows * states, LANES), jnp.float32), rates],
        name="end_state",
    )(delta, u_in, bc_proj, a_rate)
    tokens = jax.ShapeDtypeStruct((rows * groups, LANES), jnp.float32)
    spread = pltpu.VMEM((rows * states, LANES), jnp.float32)
    local = pl.pallas_call(
        local_kernel,
        out_shape=(tokens, tokens, jax.ShapeDtypeStruct((rows * states, LANES), jnp.float32)),
        in_specs=[whole()] * 4,
        out_specs=(whole(),) * 3,
        scratch_shapes=[flat, flat, spread, rates],
        cost_estimate=pl.CostEstimate(
            flops=6 * rows * channels * states,
            bytes_accessed=4 * rows * (4 * channels + states * LANES),
            transcendentals=rows * channels * states,
        ),
        name="local",
    )(delta, u_in, bc_proj, a_rate)
    ends = lax.all_to_all(ends, "ctx", split_axis=0, concat_axis=0, tiled=True)
    entering = pl.pallas_call(
        carry_kernel,
        out_shape=jax.ShapeDtypeStruct((count * groups, LANES), jnp.float32),
        in_specs=[smem, whole(), whole()],
        out_specs=whole(),
        scratch_shapes=[rates],
        name="carry",
    )(me, ends, a_rate)
    entering = lax.all_to_all(entering, "ctx", split_axis=0, concat_axis=0, tiled=True)
    gated = pl.pallas_call(
        gated_kernel,
        out_shape=jax.ShapeDtypeStruct((rows, channels), jnp.bfloat16),
        in_specs=[whole()] * 8,
        out_specs=whole(),
        scratch_shapes=[flat, rates],
        name="gated",
    )(u_in, z_in, a_rate, d_skip.reshape(1, channels), entering, *local)

    ring = [(i, (i + 2 - 4 * (i % 2)) % count) for i in range(count)]
    trade = [(i, i ^ 1) for i in range(count)]
    swapped = lax.ppermute(gated, "ctx", trade)
    gated, swapped = lax.optimization_barrier((gated, swapped))
    sources = [gated, swapped]
    for unit in range(count // 2 - 1):
        sources.append(lax.ppermute(sources[unit], "ctx", ring))
    arrived = sources[2:]
    early = len(arrived) - 3

    def place_of(unit, side):
        return side * (unit // 2 + 1), (unit % 2 == 0) == (side == -1)

    def project(blocks, places, done):
        tall = len(places) * rows
        return pl.pallas_call(
            functools.partial(project_kernel, tuple(places)),
            out_shape=jax.ShapeDtypeStruct((rows * count, width), jnp.bfloat16),
            in_specs=[smem]
            + [whole()] * (len(places) + 1)
            + [pl.BlockSpec(memory_space=pl.ANY)] * len(done),
            out_specs=pl.BlockSpec(memory_space=pl.ANY),
            scratch_shapes=[
                pltpu.VMEM((tall, channels), jnp.bfloat16),
                pltpu.VMEM((tall, width), jnp.bfloat16),
                pltpu.SemaphoreType.DMA((len(places),)),
            ],
            input_output_aliases={len(places) + 2: 0} if done else {},
            cost_estimate=pl.CostEstimate(
                flops=2 * tall * channels * width,
                bytes_accessed=2 * tall * (channels + width),
                transcendentals=0,
            ),
            name="project",
        )(me, w_out, *blocks, *done)

    blocks, places = [gated, swapped], [(0, True), (0, False)]
    for unit in range(early):
        blocks += [arrived[unit], lax.ppermute(arrived[unit], "ctx", trade)]
        places += [place_of(unit, -1), place_of(unit, 1)]
    terms = project(blocks, places, [])
    last, terms = lax.optimization_barrier((arrived[-1], terms))
    blocks, places = [], []
    for unit in range(early, len(arrived)):
        value = last if unit == len(arrived) - 1 else arrived[unit]
        blocks += [value, lax.ppermute(value, "ctx", trade)]
        places += [place_of(unit, -1), place_of(unit, 1)]
    terms = project(blocks, places, [terms])

    received = lax.all_to_all(
        terms.reshape(count, rows, width), "exp", split_axis=0, concat_axis=0
    )
    return jnp.sum(received.astype(jnp.float32), axis=0).astype(jnp.bfloat16)


def solution(mesh):
    return jax.shard_map(
        body,
        mesh=mesh,
        in_specs=(
            P("ctx", "exp"),
            P("ctx", "exp"),
            P("ctx", "exp"),
            P(None, "ctx"),
            P(None, "exp"),
            P("exp"),
            P("exp", "ctx"),
        ),
        out_specs=P("exp", "ctx"),
        check_vma=False,
    )
```

```python
import functools
import math

import jax
import jax.numpy as jnp
from jax import lax
from jax.experimental import pallas as pl
from jax.experimental.pallas import tpu as pltpu
from jax.sharding import PartitionSpec as P

LANES = 128
SUB = 8
NEG_LOG2E = -math.log2(math.e)


def fill_transposed(dst, rows, groups, make):
    for g in range(groups):
        dst[pl.ds(g, rows, stride=groups), :] = make(g)


def fill_coefficients(dst, bc, rows, count):
    turned = bc.T
    for n in range(count):
        dst[pl.ds(n, rows, stride=count), :] = jnp.broadcast_to(
            turned[:, n : n + 1], (rows, LANES)
        )


def end_state_kernel(delta_ref, u_ref, bc_ref, a_ref, out_ref, d_t, w_t, b_t, a_t):
    rows, channels = delta_ref.shape
    groups = channels // LANES
    states = a_ref.shape[0]

    def lanes(g):
        return slice(g * LANES, (g + 1) * LANES)

    fill_transposed(d_t, rows, groups, lambda g: delta_ref[:, lanes(g)])
    fill_transposed(
        w_t,
        rows,
        groups,
        lambda g: delta_ref[:, lanes(g)] * u_ref[:, lanes(g)].astype(jnp.float32),
    )
    fill_coefficients(b_t, bc_ref[:states, :], rows, states)
    fill_transposed(a_t, states, groups, lambda g: a_ref[:, lanes(g)])
    rate = [a_t[n * groups : (n + 1) * groups, :] * NEG_LOG2E for n in range(states)]

    def step(t, carry):
        total, state = carry
        d = d_t[pl.ds(pl.multiple_of(t * groups, groups), groups), :]
        w = w_t[pl.ds(pl.multiple_of(t * groups, groups), groups), :]
        new = []
        for n in range(states):
            b = b_t[pl.ds(t * states + n, groups, stride=0), :]
            new.append(jnp.exp2(d * rate[n]) * state[n] + w * b)
        return total + d, tuple(new)

    zero = jnp.zeros((groups, LANES), jnp.float32)
    total, state = lax.fori_loop(0, rows, step, (zero, (zero,) * states), unroll=8)
    for n in range(states):
        base = 2 * n * groups
        out_ref[base : base + groups, :] = state[n]
        out_ref[base + groups : base + 2 * groups, :] = total


def carry_kernel(me_ref, ends_ref, a_ref, out_ref, rate_t):
    count = ends_ref.shape[0] // (2 * SUB)
    fill_transposed(
        rate_t, a_ref.shape[0], SUB, lambda g: a_ref[:, g * LANES : (g + 1) * LANES] * NEG_LOG2E
    )
    rate = rate_t[pl.ds(pl.multiple_of(me_ref[0] * SUB, SUB), SUB), :]
    state = jnp.zeros((SUB, LANES), jnp.float32)
    for k in range(count):
        out_ref[k * SUB : (k + 1) * SUB, :] = state
        base = 2 * k * SUB
        total = ends_ref[base + SUB : base + 2 * SUB, :]
        state = jnp.exp2(total * rate) * state + ends_ref[base : base + SUB, :]


def local_kernel(delta_ref, u_ref, bc_ref, a_ref, y_ref, sum_ref, c_ref, d_t, w_t, b_t, a_t):
    rows, channels = delta_ref.shape
    groups = channels // LANES
    states = a_ref.shape[0]

    def lanes(g):
        return slice(g * LANES, (g + 1) * LANES)

    fill_transposed(d_t, rows, groups, lambda g: delta_ref[:, lanes(g)])
    fill_transposed(
        w_t,
        rows,
        groups,
        lambda g: delta_ref[:, lanes(g)] * u_ref[:, lanes(g)].astype(jnp.float32),
    )
    fill_coefficients(b_t, bc_ref[:states, :], rows, states)
    fill_coefficients(c_ref, bc_ref[states:, :], rows, states)
    fill_transposed(a_t, states, groups, lambda g: a_ref[:, lanes(g)])
    rate = [a_t[n * groups : (n + 1) * groups, :] * NEG_LOG2E for n in range(states)]

    def step(t, carry):
        total, state = carry
        at = pl.ds(pl.multiple_of(t * groups, groups), groups)
        d = d_t[at, :]
        w = w_t[at, :]
        new = []
        parts = [None] * 4
        for n in range(states):
            b = b_t[pl.ds(t * states + n, groups, stride=0), :]
            c = c_ref[pl.ds(t * states + n, groups, stride=0), :]
            s = jnp.exp2(d * rate[n]) * state[n] + w * b
            new.append(s)
            term = s * c
            parts[n % 4] = term if parts[n % 4] is None else parts[n % 4] + term
        y_ref[at, :] = (parts[0] + parts[1]) + (parts[2] + parts[3])
        total = total + d
        sum_ref[at, :] = total
        return total, tuple(new)

    zero = jnp.zeros((groups, LANES), jnp.float32)
    lax.fori_loop(0, rows, step, (zero, (zero,) * states), unroll=4)


def gated_kernel(
    u_ref, z_ref, a_ref, skip_ref, start_ref, y_ref, sum_ref, c_ref, out_ref, y_t, a_t
):
    rows, channels = u_ref.shape
    groups = channels // LANES
    states = a_ref.shape[0]

    def lanes(g):
        return slice(g * LANES, (g + 1) * LANES)

    fill_transposed(a_t, states, groups, lambda g: a_ref[:, lanes(g)])
    rate = [a_t[n * groups : (n + 1) * groups, :] * NEG_LOG2E for n in range(states)]
    start = [start_ref[n * groups : (n + 1) * groups, :] for n in range(states)]

    def step(t, carry):
        at = pl.ds(pl.multiple_of(t * groups, groups), groups)
        total = sum_ref[at, :]
        parts = [None] * 4
        for n in range(states):
            c = c_ref[pl.ds(t * states + n, groups, stride=0), :]
            term = jnp.exp2(total * rate[n]) * start[n] * c
            parts[n % 4] = term if parts[n % 4] is None else parts[n % 4] + term
        y_t[at, :] = y_ref[at, :] + ((parts[0] + parts[1]) + (parts[2] + parts[3]))
        return carry

    lax.fori_loop(0, rows, step, 0, unroll=8)

    for g in range(groups):
        y = y_t[pl.ds(g, rows, stride=groups), :]
        u = u_ref[:, lanes(g)].astype(jnp.float32)
        z = z_ref[:, lanes(g)].astype(jnp.float32)
        mixed = y + skip_ref[:, lanes(g)] * u
        out_ref[:, lanes(g)] = (mixed * (z / (1.0 + jnp.exp(-z)))).astype(jnp.bfloat16)


def project_kernel(places, me_ref, w_ref, *refs):
    units = len(places)
    blocks, out_ref, joined, result, sems = refs[:units], *refs[-4:]
    rows = blocks[0].shape[0]
    count = out_ref.shape[0] // rows
    me = me_ref[0]
    core = lax.rem(me, 2)
    way = 2 - 4 * core
    copies = []
    for first in range(0, units, 2):
        piece = slice(first * rows, (first + 2) * rows)
        joined[first * rows : (first + 1) * rows, :] = blocks[first][...]
        joined[(first + 1) * rows : (first + 2) * rows, :] = blocks[first + 1][...]
        result[piece, :] = jnp.dot(
            joined[piece, :], w_ref[...], preferred_element_type=jnp.float32
        ).astype(jnp.bfloat16)
        for i in (first, first + 1):
            step, same = places[i]
            home = me - core + step * way + (core if same else 1 - core)
            at = pl.multiple_of(lax.rem(home + 2 * count, count) * rows, rows)
            copies.append(
                pltpu.make_async_copy(
                    result.at[pl.ds(i * rows, rows), :], out_ref.at[pl.ds(at, rows), :], sems.at[i]
                )
            )
            copies[-1].start()
    for copy in copies:
        copy.wait()


def whole():
    return pl.BlockSpec(memory_space=pltpu.VMEM)


def body(u_in, z_in, delta, bc_proj, a_rate, d_skip, w_out):
    rows, channels = u_in.shape
    states = a_rate.shape[0]
    groups = channels // LANES
    width = w_out.shape[1]
    count = lax.axis_size("ctx")
    flat = pltpu.VMEM((rows * groups, LANES), jnp.float32)
    rates = pltpu.VMEM((states * groups, LANES), jnp.float32)
    smem = pl.BlockSpec(memory_space=pltpu.SMEM)
    me = lax.axis_index("ctx").astype(jnp.int32).reshape(1)

    ends = pl.pallas_call(
        end_state_kernel,
        out_shape=jax.ShapeDtypeStruct((2 * states * groups, LANES), jnp.float32),
        in_specs=[whole()] * 4,
        out_specs=whole(),
        scratch_shapes=[flat, flat, pltpu.VMEM((rows * states, LANES), jnp.float32), rates],
        name="end_state",
    )(delta, u_in, bc_proj, a_rate)
    tokens = jax.ShapeDtypeStruct((rows * groups, LANES), jnp.float32)
    spread = pltpu.VMEM((rows * states, LANES), jnp.float32)
    local = pl.pallas_call(
        local_kernel,
        out_shape=(tokens, tokens, jax.ShapeDtypeStruct((rows * states, LANES), jnp.float32)),
        in_specs=[whole()] * 4,
        out_specs=(whole(),) * 3,
        scratch_shapes=[flat, flat, spread, rates],
        cost_estimate=pl.CostEstimate(
            flops=6 * rows * channels * states,
            bytes_accessed=4 * rows * (4 * channels + states * LANES),
            transcendentals=rows * channels * states,
        ),
        name="local",
    )(delta, u_in, bc_proj, a_rate)
    ends = lax.all_to_all(ends, "ctx", split_axis=0, concat_axis=0, tiled=True)
    entering = pl.pallas_call(
        carry_kernel,
        out_shape=jax.ShapeDtypeStruct((count * groups, LANES), jnp.float32),
        in_specs=[smem, whole(), whole()],
        out_specs=whole(),
        scratch_shapes=[rates],
        name="carry",
    )(me, ends, a_rate)
    entering = lax.all_to_all(entering, "ctx", split_axis=0, concat_axis=0, tiled=True)
    gated = pl.pallas_call(
        gated_kernel,
        out_shape=jax.ShapeDtypeStruct((rows, channels), jnp.bfloat16),
        in_specs=[whole()] * 8,
        out_specs=whole(),
        scratch_shapes=[flat, rates],
        name="gated",
    )(u_in, z_in, a_rate, d_skip.reshape(1, channels), entering, *local)

    ring = [(i, (i + 2 - 4 * (i % 2)) % count) for i in range(count)]
    trade = [(i, i ^ 1) for i in range(count)]
    swapped = lax.ppermute(gated, "ctx", trade)
    gated, swapped = lax.optimization_barrier((gated, swapped))
    sources = [gated, swapped]
    for unit in range(count // 2 - 1):
        sources.append(lax.ppermute(sources[unit], "ctx", ring))
    arrived = sources[2:]
    early = len(arrived) - 3

    def place_of(unit, side):
        return side * (unit // 2 + 1), (unit % 2 == 0) == (side == -1)

    def project(blocks, places, done):
        tall = len(places) * rows
        return pl.pallas_call(
            functools.partial(project_kernel, tuple(places)),
            out_shape=jax.ShapeDtypeStruct((rows * count, width), jnp.bfloat16),
            in_specs=[smem]
            + [whole()] * (len(places) + 1)
            + [pl.BlockSpec(memory_space=pl.ANY)] * len(done),
            out_specs=pl.BlockSpec(memory_space=pl.ANY),
            scratch_shapes=[
                pltpu.VMEM((tall, channels), jnp.bfloat16),
                pltpu.VMEM((tall, width), jnp.bfloat16),
                pltpu.SemaphoreType.DMA((len(places),)),
            ],
            input_output_aliases={len(places) + 2: 0} if done else {},
            cost_estimate=pl.CostEstimate(
                flops=2 * tall * channels * width,
                bytes_accessed=2 * tall * (channels + width),
                transcendentals=0,
            ),
            name="project",
        )(me, w_out, *blocks, *done)

    blocks, places = [gated, swapped], [(0, True), (0, False)]
    for unit in range(early):
        blocks += [arrived[unit], lax.ppermute(arrived[unit], "ctx", trade)]
        places += [place_of(unit, -1), place_of(unit, 1)]
    terms = project(blocks, places, [])
    last, terms = lax.optimization_barrier((arrived[-1], terms))
    blocks, places = [], []
    for unit in range(early, len(arrived)):
        value = last if unit == len(arrived) - 1 else arrived[unit]
        blocks += [value, lax.ppermute(value, "ctx", trade)]
        places += [place_of(unit, -1), place_of(unit, 1)]
    terms = project(blocks, places, [terms])

    received = lax.all_to_all(
        terms.reshape(count, rows, width), "exp", split_axis=0, concat_axis=0
    )
    return jnp.sum(received.astype(jnp.float32), axis=0).astype(jnp.bfloat16)


def solution(mesh):
    return jax.shard_map(
        body,
        mesh=mesh,
        in_specs=(
            P("ctx", "exp"),
            P("ctx", "exp"),
            P("ctx", "exp"),
            P(None, "ctx"),
            P(None, "exp"),
            P("exp"),
            P("exp", "ctx"),
        ),
        out_specs=P("exp", "ctx"),
        check_vma=False,
    )
```

```python
import functools
import math

import jax
import jax.numpy as jnp
from jax import lax
from jax.experimental import pallas as pl
from jax.experimental.pallas import tpu as pltpu
from jax.sharding import PartitionSpec as P

LANES = 128
SUB = 8
NEG_LOG2E = -math.log2(math.e)


def fill_transposed(dst, rows, groups, make):
    for g in range(groups):
        dst[pl.ds(g, rows, stride=groups), :] = make(g)


def fill_coefficients(dst, bc, rows, count):
    turned = bc.T
    for n in range(count):
        dst[pl.ds(n, rows, stride=count), :] = jnp.broadcast_to(
            turned[:, n : n + 1], (rows, LANES)
        )


def end_state_kernel(delta_ref, u_ref, bc_ref, a_ref, out_ref, d_t, w_t, b_t, a_t):
    rows, channels = delta_ref.shape
    groups = channels // LANES
    states = a_ref.shape[0]

    def lanes(g):
        return slice(g * LANES, (g + 1) * LANES)

    fill_transposed(d_t, rows, groups, lambda g: delta_ref[:, lanes(g)])
    fill_transposed(
        w_t,
        rows,
        groups,
        lambda g: delta_ref[:, lanes(g)] * u_ref[:, lanes(g)].astype(jnp.float32),
    )
    fill_coefficients(b_t, bc_ref[:states, :], rows, states)
    fill_transposed(a_t, states, groups, lambda g: a_ref[:, lanes(g)])
    rate = [a_t[n * groups : (n + 1) * groups, :] * NEG_LOG2E for n in range(states)]

    def step(t, carry):
        total, state = carry
        d = d_t[pl.ds(pl.multiple_of(t * groups, groups), groups), :]
        w = w_t[pl.ds(pl.multiple_of(t * groups, groups), groups), :]
        new = []
        for n in range(states):
            b = b_t[pl.ds(t * states + n, groups, stride=0), :]
            new.append(jnp.exp2(d * rate[n]) * state[n] + w * b)
        return total + d, tuple(new)

    zero = jnp.zeros((groups, LANES), jnp.float32)
    total, state = lax.fori_loop(0, rows, step, (zero, (zero,) * states), unroll=8)
    for n in range(states):
        base = 2 * n * groups
        out_ref[base : base + groups, :] = state[n]
        out_ref[base + groups : base + 2 * groups, :] = total


def carry_kernel(me_ref, ends_ref, a_ref, out_ref, rate_t):
    count = ends_ref.shape[0] // (2 * SUB)
    fill_transposed(
        rate_t, a_ref.shape[0], SUB, lambda g: a_ref[:, g * LANES : (g + 1) * LANES] * NEG_LOG2E
    )
    rate = rate_t[pl.ds(pl.multiple_of(me_ref[0] * SUB, SUB), SUB), :]
    state = jnp.zeros((SUB, LANES), jnp.float32)
    for k in range(count):
        out_ref[k * SUB : (k + 1) * SUB, :] = state
        base = 2 * k * SUB
        total = ends_ref[base + SUB : base + 2 * SUB, :]
        state = jnp.exp2(total * rate) * state + ends_ref[base : base + SUB, :]


def local_kernel(delta_ref, u_ref, bc_ref, a_ref, y_ref, sum_ref, c_ref, d_t, w_t, b_t, a_t):
    rows, channels = delta_ref.shape
    groups = channels // LANES
    states = a_ref.shape[0]

    def lanes(g):
        return slice(g * LANES, (g + 1) * LANES)

    fill_transposed(d_t, rows, groups, lambda g: delta_ref[:, lanes(g)])
    fill_transposed(
        w_t,
        rows,
        groups,
        lambda g: delta_ref[:, lanes(g)] * u_ref[:, lanes(g)].astype(jnp.float32),
    )
    fill_coefficients(b_t, bc_ref[:states, :], rows, states)
    fill_coefficients(c_ref, bc_ref[states:, :], rows, states)
    fill_transposed(a_t, states, groups, lambda g: a_ref[:, lanes(g)])
    rate = [a_t[n * groups : (n + 1) * groups, :] * NEG_LOG2E for n in range(states)]

    def step(t, carry):
        total, state = carry
        at = pl.ds(pl.multiple_of(t * groups, groups), groups)
        d = d_t[at, :]
        w = w_t[at, :]
        new = []
        parts = [None] * 4
        for n in range(states):
            b = b_t[pl.ds(t * states + n, groups, stride=0), :]
            c = c_ref[pl.ds(t * states + n, groups, stride=0), :]
            s = jnp.exp2(d * rate[n]) * state[n] + w * b
            new.append(s)
            term = s * c
            parts[n % 4] = term if parts[n % 4] is None else parts[n % 4] + term
        y_ref[at, :] = (parts[0] + parts[1]) + (parts[2] + parts[3])
        total = total + d
        sum_ref[at, :] = total
        return total, tuple(new)

    zero = jnp.zeros((groups, LANES), jnp.float32)
    lax.fori_loop(0, rows, step, (zero, (zero,) * states), unroll=4)


def gated_kernel(
    u_ref, z_ref, a_ref, skip_ref, start_ref, y_ref, sum_ref, c_ref, out_ref, y_t, a_t
):
    rows, channels = u_ref.shape
    groups = channels // LANES
    states = a_ref.shape[0]

    def lanes(g):
        return slice(g * LANES, (g + 1) * LANES)

    fill_transposed(a_t, states, groups, lambda g: a_ref[:, lanes(g)])
    rate = [a_t[n * groups : (n + 1) * groups, :] * NEG_LOG2E for n in range(states)]
    start = [start_ref[n * groups : (n + 1) * groups, :] for n in range(states)]

    def step(t, carry):
        at = pl.ds(pl.multiple_of(t * groups, groups), groups)
        total = sum_ref[at, :]
        parts = [None] * 4
        for n in range(states):
            c = c_ref[pl.ds(t * states + n, groups, stride=0), :]
            term = jnp.exp2(total * rate[n]) * start[n] * c
            parts[n % 4] = term if parts[n % 4] is None else parts[n % 4] + term
        y_t[at, :] = y_ref[at, :] + ((parts[0] + parts[1]) + (parts[2] + parts[3]))
        return carry

    lax.fori_loop(0, rows, step, 0, unroll=8)

    for g in range(groups):
        y = y_t[pl.ds(g, rows, stride=groups), :]
        u = u_ref[:, lanes(g)].astype(jnp.float32)
        z = z_ref[:, lanes(g)].astype(jnp.float32)
        mixed = y + skip_ref[:, lanes(g)] * u
        out_ref[:, lanes(g)] = (mixed * (z / (1.0 + jnp.exp(-z)))).astype(jnp.bfloat16)


def project_kernel(places, me_ref, w_ref, *refs):
    units = len(places)
    blocks, out_ref, joined, result, sems = refs[:units], *refs[-4:]
    rows = blocks[0].shape[0]
    count = out_ref.shape[0] // rows
    me = me_ref[0]
    core = lax.rem(me, 2)
    way = 2 - 4 * core
    copies = []
    for first in range(0, units, 2):
        piece = slice(first * rows, (first + 2) * rows)
        joined[first * rows : (first + 1) * rows, :] = blocks[first][...]
        joined[(first + 1) * rows : (first + 2) * rows, :] = blocks[first + 1][...]
        result[piece, :] = jnp.dot(
            joined[piece, :], w_ref[...], preferred_element_type=jnp.float32
        ).astype(jnp.bfloat16)
        for i in (first, first + 1):
            step, same = places[i]
            home = me - core + step * way + (core if same else 1 - core)
            at = pl.multiple_of(lax.rem(home + 2 * count, count) * rows, rows)
            copies.append(
                pltpu.make_async_copy(
                    result.at[pl.ds(i * rows, rows), :], out_ref.at[pl.ds(at, rows), :], sems.at[i]
                )
            )
            copies[-1].start()
    for copy in copies:
        copy.wait()


def whole():
    return pl.BlockSpec(memory_space=pltpu.VMEM)


def body(u_in, z_in, delta, bc_proj, a_rate, d_skip, w_out):
    rows, channels = u_in.shape
    states = a_rate.shape[0]
    groups = channels // LANES
    width = w_out.shape[1]
    count = lax.axis_size("ctx")
    flat = pltpu.VMEM((rows * groups, LANES), jnp.float32)
    rates = pltpu.VMEM((states * groups, LANES), jnp.float32)
    smem = pl.BlockSpec(memory_space=pltpu.SMEM)
    me = lax.axis_index("ctx").astype(jnp.int32).reshape(1)

    ends = pl.pallas_call(
        end_state_kernel,
        out_shape=jax.ShapeDtypeStruct((2 * states * groups, LANES), jnp.float32),
        in_specs=[whole()] * 4,
        out_specs=whole(),
        scratch_shapes=[flat, flat, pltpu.VMEM((rows * states, LANES), jnp.float32), rates],
        name="end_state",
    )(delta, u_in, bc_proj, a_rate)
    tokens = jax.ShapeDtypeStruct((rows * groups, LANES), jnp.float32)
    spread = pltpu.VMEM((rows * states, LANES), jnp.float32)
    local = pl.pallas_call(
        local_kernel,
        out_shape=(tokens, tokens, jax.ShapeDtypeStruct((rows * states, LANES), jnp.float32)),
        in_specs=[whole()] * 4,
        out_specs=(whole(),) * 3,
        scratch_shapes=[flat, flat, spread, rates],
        cost_estimate=pl.CostEstimate(
            flops=6 * rows * channels * states,
            bytes_accessed=4 * rows * (4 * channels + states * LANES),
            transcendentals=rows * channels * states,
        ),
        name="local",
    )(delta, u_in, bc_proj, a_rate)
    ends = lax.all_to_all(ends, "ctx", split_axis=0, concat_axis=0, tiled=True)
    entering = pl.pallas_call(
        carry_kernel,
        out_shape=jax.ShapeDtypeStruct((count * groups, LANES), jnp.float32),
        in_specs=[smem, whole(), whole()],
        out_specs=whole(),
        scratch_shapes=[rates],
        name="carry",
    )(me, ends, a_rate)
    entering = lax.all_to_all(entering, "ctx", split_axis=0, concat_axis=0, tiled=True)
    gated = pl.pallas_call(
        gated_kernel,
        out_shape=jax.ShapeDtypeStruct((rows, channels), jnp.bfloat16),
        in_specs=[whole()] * 8,
        out_specs=whole(),
        scratch_shapes=[flat, rates],
        name="gated",
    )(u_in, z_in, a_rate, d_skip.reshape(1, channels), entering, *local)

    ring = [(i, (i + 2 - 4 * (i % 2)) % count) for i in range(count)]
    trade = [(i, i ^ 1) for i in range(count)]
    swapped = lax.ppermute(gated, "ctx", trade)
    gated, swapped = lax.optimization_barrier((gated, swapped))
    sources = [gated, swapped]
    for unit in range(count // 2 - 1):
        sources.append(lax.ppermute(sources[unit], "ctx", ring))
    arrived = sources[2:]
    early = len(arrived) - 3

    def place_of(unit, side):
        return side * (unit // 2 + 1), (unit % 2 == 0) == (side == -1)

    def project(blocks, places, done):
        tall = len(places) * rows
        return pl.pallas_call(
            functools.partial(project_kernel, tuple(places)),
            out_shape=jax.ShapeDtypeStruct((rows * count, width), jnp.bfloat16),
            in_specs=[smem]
            + [whole()] * (len(places) + 1)
            + [pl.BlockSpec(memory_space=pl.ANY)] * len(done),
            out_specs=pl.BlockSpec(memory_space=pl.ANY),
            scratch_shapes=[
                pltpu.VMEM((tall, channels), jnp.bfloat16),
                pltpu.VMEM((tall, width), jnp.bfloat16),
                pltpu.SemaphoreType.DMA((len(places),)),
            ],
            input_output_aliases={len(places) + 2: 0} if done else {},
            cost_estimate=pl.CostEstimate(
                flops=2 * tall * channels * width,
                bytes_accessed=2 * tall * (channels + width),
                transcendentals=0,
            ),
            name="project",
        )(me, w_out, *blocks, *done)

    blocks, places = [gated, swapped], [(0, True), (0, False)]
    for unit in range(early):
        blocks += [arrived[unit], lax.ppermute(arrived[unit], "ctx", trade)]
        places += [place_of(unit, -1), place_of(unit, 1)]
    blocks += arrived[early:-1]
    places += [place_of(unit, -1) for unit in range(early, len(arrived) - 1)]
    terms = project(blocks, places, [])
    last, terms = lax.optimization_barrier((arrived[-1], terms))
    blocks, places = [last], [place_of(len(arrived) - 1, -1)]
    for unit in range(early, len(arrived)):
        value = last if unit == len(arrived) - 1 else arrived[unit]
        blocks.append(lax.ppermute(value, "ctx", trade))
        places.append(place_of(unit, 1))
    terms = project(blocks, places, [terms])

    received = lax.all_to_all(
        terms.reshape(count, rows, width), "exp", split_axis=0, concat_axis=0
    )
    return jnp.sum(received.astype(jnp.float32), axis=0).astype(jnp.bfloat16)


def solution(mesh):
    return jax.shard_map(
        body,
        mesh=mesh,
        in_specs=(
            P("ctx", "exp"),
            P("ctx", "exp"),
            P("ctx", "exp"),
            P(None, "ctx"),
            P(None, "exp"),
            P("exp"),
            P("exp", "ctx"),
        ),
        out_specs=P("exp", "ctx"),
        check_vma=False,
    )
```
